32 devices in a mesh: shard: 8 (over y, x, core), rep: 4 (over z).
Axes of the slice: x: 2, y: 2, z: 4, core: 2. Of those that a mesh axis runs over, the one named last changes fastest.
Arguments:
- hidden_in: bfloat16 [32, 1024, 1024], P(('shard', 'rep')), may hold values from -6 to 6
- enc_states: bfloat16 [32, 1024, 1024], P(('shard', 'rep')), may hold values from -6 to 6
- cotangent: bfloat16 [32, 1024, 1024], P(('shard', 'rep')), may hold values from -6 to 6
- prefix_len: int32 [32], P(('shard', 'rep')), may hold values from 102 to 512, as said below
- adapter_ids: int32 [32], P(('shard', 'rep')), may hold values from 0 to 7
- self_qkv: bfloat16 [3, 1024, 1024], P(None, 'shard'), may hold values from -0.25 to 0.25
- self_out: bfloat16 [1024, 1024], P('shard'), may hold values from -1.5 to 1.5
- cross_qkv: bfloat16 [3, 1024, 1024], P(None, 'shard'), may hold values from -0.25 to 0.25
- cross_out: bfloat16 [1024, 1024], P('shard'), may hold values from -1.5 to 1.5
- expand_weight: bfloat16 [1024, 4096], P('shard'), may hold values from -0.1875 to 0.1875
- reduce_weight: bfloat16 [4096, 1024], P('shard'), may hold values from -0.125 to 0.125
- attention_adapters: bfloat16 [8, 2, 8, 16, 1024], P(None, None, None, None, 'shard'), may hold values from -0.1875 to 0.1875
- narrow_adapters: bfloat16 [2, 8, 16, 1024], P(None, None, None, 'shard'), may hold values from -0.1875 to 0.1875
- wide_adapters: bfloat16 [2, 8, 16, 4096], P(None, None, None, 'shard'), may hold values from -0.09375 to 0.09375
- norm_gains: float32 [3, 1024], replicated, may hold values from 0.5 to 1.5
- norm_shifts: float32 [3, 1024], replicated, may hold values from -1 to 1
Outputs:
- layer_out: bfloat16 [32, 1024, 1024], P(('shard', 'rep'))
- hidden_grad: float32 [32, 1024, 1024], P(('shard', 'rep'))
- encoder_grad: float32 [32, 1024, 1024], P(('shard', 'rep'))
- attention_grad: float32 [8, 2, 8, 16, 1024], P(None, None, None, None, 'shard')
- narrow_grad: float32 [2, 8, 16, 1024], P(None, None, None, 'shard')
- wide_grad: float32 [2, 8, 16, 4096], P(None, None, None, 'shard')
The draws below stay inside these ranges and needn't reach their ends.
Inputs may be any that keep to these rules, and one draw needn't show every extreme that they name: `prefix_len`: some sequence has the largest and some the smallest value.
All inputs are finite; a program needn't handle non-finite values.
Results may differ from the reference program's by a relative error of at most 0.03.
The reference program's roundings to bfloat16 on the way count: a program that leaves them out, or rounds other values in their place, can miss the bound.
Values may be sent and summed in bfloat16 or wider, within the bound.
No kernel may reach another device: no remote copies, remote signals or barrier semaphores. Data moves between devices by JAX's collectives and lax.ppermute only.
A program may use at most 256 MiB of HBM per device.

```python
import jax
import jax.numpy as jnp
from jax import lax

D = 1024
HEADS = 16
HEAD_DIM = 64
FF = 4096
RANK = 16
ADAPTERS = 8
SEQ_LEN = 1024
ENC_LEN = 1024
SEQS = 32


def draw_prefix_len(key, part):
    low_end = SEQ_LEN // 10
    high_end = SEQ_LEN // 2
    subkeys = jax.random.split(key, 3)
    values = jax.random.randint(subkeys[0], (SEQS,), low_end, high_end + 1)
    high_slot = jax.random.randint(subkeys[1], (), 0, SEQS)
    low_slot = (high_slot + 1 + jax.random.randint(subkeys[2], (), 0, SEQS - 1)) % SEQS
    values = values.at[high_slot].set(high_end).at[low_slot].set(low_end)
    return values.astype(jnp.int32)


def with_ends(entries, rng, least, high):
    longest = entries.shape.index(max(entries.shape))
    spots = []
    for shift in (0, 1):
        where = [jax.random.randint(jax.random.fold_in(rng, axis), (), 0, length) for axis, length in enumerate(entries.shape)]
        where[longest] = (where[longest] + shift) % entries.shape[longest]
        spots.append(tuple(where))
    return entries.at[spots[0]].set(least).at[spots[1]].set(high)


def block_levels(rng, dims, cuts, low, top_value):
    loudness = 1.0
    for axis_at, shards_of in cuts:
        steps = jax.random.uniform(jax.random.fold_in(jax.random.fold_in(rng, 6), axis_at), (shards_of,), jnp.float32, low / len(cuts), top_value / len(cuts))
        loudness = loudness * jnp.repeat(jnp.exp(steps), dims[axis_at] // shards_of).reshape((-1,) + (1,) * (len(dims) - 1 - axis_at))
    return loudness


def bell_draw(own_key, extent, scale, most, shards=(), kind=jnp.bfloat16):
    loudness = block_levels(own_key, extent, shards, -0.22, 0.18) if shards else 1.0
    values = jax.random.normal(own_key, extent, jnp.float32) * scale * loudness
    return jnp.minimum(jnp.maximum(values, -most), most).astype(kind)


def setup_inputs(seed: int = 0) -> dict:
    key_of = jax.random.split(jax.random.key(seed), 17)
    return {
        "hidden_in": bell_draw(key_of[0], (SEQS, SEQ_LEN, D), 1.0, 6.0, ((0, 32),)),
        "enc_states": bell_draw(key_of[1], (SEQS, ENC_LEN, D), 1.0, 6.0, ((0, 32),)),
        "cotangent": bell_draw(key_of[2], (SEQS, SEQ_LEN, D), 1.0, 6.0, ((0, 32),)),
        "prefix_len": draw_prefix_len(jax.random.fold_in(key_of[16], 71), 0),
        "adapter_ids": with_ends(jax.random.randint(key_of[4], (SEQS,), 0, ADAPTERS), jax.random.fold_in(key_of[4], 1), 0, ADAPTERS - 1).astype(jnp.int32),
        "self_qkv": bell_draw(key_of[5], (3, D, D), (D // 2) ** -0.5, 0.25, ((1, 8),)),
        "self_out": bell_draw(key_of[6], (D, D), (D // 64) ** -0.5, 1.5, ((0, 8),)),
        "cross_qkv": bell_draw(key_of[7], (3, D, D), (D // 2) ** -0.5, 0.25, ((1, 8),)),
        "cross_out": bell_draw(key_of[8], (D, D), (D // 64) ** -0.5, 1.5, ((0, 8),)),
        "expand_weight": bell_draw(key_of[9], (D, FF), D ** -0.5, 0.1875, ((0, 8),)),
        "reduce_weight": bell_draw(key_of[10], (FF, D), (FF // 2) ** -0.5, 0.125, ((0, 8),)),
        "attention_adapters": bell_draw(key_of[11], (8, 2, ADAPTERS, RANK, D), D ** -0.5, 0.1875, ((4, 8),)),
        "narrow_adapters": bell_draw(key_of[12], (2, ADAPTERS, RANK, D), D ** -0.5, 0.1875, ((3, 8),)),
        "wide_adapters": bell_draw(key_of[13], (2, ADAPTERS, RANK, FF), FF ** -0.5, 0.09375, ((3, 8),)),
        "norm_gains": jnp.clip(1.0 + 0.1 * jax.random.normal(key_of[14], (3, D), jnp.float32), 0.5, 1.5),
        "norm_shifts": bell_draw(key_of[15], (3, D), 0.2, 1.0, (), jnp.float32),
    }


@jax.custom_vjp
def low(v):
    return lax.optimization_barrier(v.astype(jnp.bfloat16)).astype(jnp.float32)

@jax.custom_vjp
def low_back(v):
    return v

def low_keep(v):
    return (low(v), None)

def low_pass(kept, grad):
    return (grad,)

def back_keep(v):
    return (v, None)

def back_low(kept, grad):
    return (low(grad),)
low.defvjp(low_keep, low_pass)
low_back.defvjp(back_keep, back_low)
adapter_scale = 2.0
norm_eps = 1e-05
masked_score = -1000000000.0

def round_both(value):
    return low(low_back(value))

def matmul(left, right):
    return jnp.dot(left, right, precision=lax.Precision.HIGHEST)

def project(inputs, weight, down_rows, up_rows):
    reduced = round_both(matmul(inputs, down_rows.T))
    return matmul(inputs, weight) + adapter_scale * matmul(reduced, up_rows)

def layer_norm(values, gain, shift):
    center = values - lax.optimization_barrier(jnp.mean(values, axis=-1, keepdims=True))
    variance = lax.optimization_barrier(jnp.mean(center * center, axis=-1, keepdims=True))
    return center * lax.rsqrt(variance + norm_eps) * gain + shift

def split_heads(matrix):
    return matrix.reshape(matrix.shape[0], HEADS // 2, 2, HEAD_DIM).transpose(1, 2, 0, 3)

def attend(queries, keys_in, values_in, allowed):
    row_count = queries.shape[0]
    score_scale = HEAD_DIM ** (-0.5)

    def one_pair(operands):
        query_pair, key_pair, value_pair = operands
        scores = jnp.einsum('hqd,hkd->hqk', query_pair, key_pair, precision=lax.Precision.HIGHEST) * score_scale
        scores = low_back(jnp.where(allowed[None], scores, masked_score))
        probs = low(jax.nn.softmax(scores, axis=-1))
        return jnp.einsum('hqk,hkd->hqd', probs, value_pair, precision=lax.Precision.HIGHEST)
    mixed = lax.map(jax.checkpoint(one_pair), (split_heads(queries), split_heads(keys_in), split_heads(values_in)))
    return mixed.transpose(2, 0, 1, 3).reshape(row_count, HEADS * HEAD_DIM)

def forward(hidden, encoder, attention_full, narrow_full, wide_full, chosen, prefix, frozen):
    self_qkv, self_out, cross_qkv, cross_out, expand_weight, reduce_weight, norm_gains, norm_shifts = frozen
    attn_sel = lax.dynamic_index_in_dim(attention_full, chosen, 2, keepdims=False)
    narrow_sel = lax.dynamic_index_in_dim(narrow_full, chosen, 1, keepdims=False)
    wide_sel = lax.dynamic_index_in_dim(wide_full, chosen, 1, keepdims=False)
    positions = jnp.arange(SEQ_LEN, dtype=jnp.int32)
    allowed = (positions[None, :] <= positions[:, None]) | (positions[None, :] < prefix)
    cross_allowed = jnp.ones((SEQ_LEN, ENC_LEN), dtype=jnp.bool_)
    hidden_low = low(hidden)
    queries = round_both(project(hidden_low, self_qkv[0], attn_sel[0, 0], attn_sel[0, 1]))
    keys_in = round_both(project(hidden_low, self_qkv[1], attn_sel[1, 0], attn_sel[1, 1]))
    values_in = round_both(project(hidden_low, self_qkv[2], attn_sel[2, 0], attn_sel[2, 1]))
    mixed = round_both(attend(queries, keys_in, values_in, allowed))
    branch = low_back(project(mixed, self_out, attn_sel[3, 0], attn_sel[3, 1]))
    after_self = layer_norm(hidden + branch, norm_gains[0], norm_shifts[0])
    cross_in = low(after_self)
    encoder_low = low(encoder)
    cross_queries = round_both(project(cross_in, cross_qkv[0], attn_sel[4, 0], attn_sel[4, 1]))
    cross_keys = round_both(project(encoder_low, cross_qkv[1], attn_sel[5, 0], attn_sel[5, 1]))
    cross_values = round_both(project(encoder_low, cross_qkv[2], attn_sel[6, 0], attn_sel[6, 1]))
    cross_mixed = round_both(attend(cross_queries, cross_keys, cross_values, cross_allowed))
    cross_branch = low_back(project(cross_mixed, cross_out, attn_sel[7, 0], attn_sel[7, 1]))
    after_cross = layer_norm(after_self + cross_branch, norm_gains[1], norm_shifts[1])
    expanded = low_back(project(low(after_cross), expand_weight, narrow_sel[0], wide_sel[0]))
    active = round_both(jax.nn.gelu(expanded, approximate=False))
    feed_branch = low_back(project(active, reduce_weight, wide_sel[1], narrow_sel[1]))
    return layer_norm(after_cross + feed_branch, norm_gains[2], norm_shifts[2])

def reference(hidden_in, enc_states, cotangent, prefix_len, adapter_ids, self_qkv, self_out, cross_qkv, cross_out, expand_weight, reduce_weight, attention_adapters, narrow_adapters, wide_adapters, norm_gains, norm_shifts):
    frozen = tuple((member.astype(jnp.float32) for member in (self_qkv, self_out, cross_qkv, cross_out, expand_weight, reduce_weight, norm_gains, norm_shifts)))
    adapters = tuple((member.astype(jnp.float32) for member in (attention_adapters, narrow_adapters, wide_adapters)))

    def per_sequence(running, inputs):
        hidden, encoder, upstream, prefix, chosen = inputs

        def run(hidden_f, encoder_f, attention_full, narrow_full, wide_full):
            return forward(hidden_f, encoder_f, attention_full, narrow_full, wide_full, chosen, prefix, frozen)
        result, pullback = jax.vjp(run, hidden.astype(jnp.float32), encoder.astype(jnp.float32), *adapters)
        grads = pullback(upstream.astype(jnp.float32))
        running = tuple((total_now + partial_value for total_now, partial_value in zip(running, grads[2:])))
        return (running, (result.astype(jnp.bfloat16), grads[0], grads[1]))
    zeros_start = tuple((jnp.zeros_like(member) for member in adapters))
    running, (outputs, hidden_grads, encoder_grads) = lax.scan(per_sequence, zeros_start, (hidden_in, enc_states, cotangent, prefix_len, adapter_ids))
    return (outputs, hidden_grads, encoder_grads, running[0], running[1], running[2])
```

```python
import functools

import jax
import jax.numpy as jnp
from jax import lax
from jax.experimental import pallas as pl
from jax.experimental.pallas import tpu as pltpu
from jax.sharding import PartitionSpec as P

HEADS = 16
HEAD_DIM = 64


adapter_scale = 2.0
norm_eps = 1e-05
masked_score = -1000000000.0


def layer_norm(values, gain, shift):
    center = values - jnp.mean(values, axis=-1, keepdims=True)
    variance = jnp.mean(center * center, axis=-1, keepdims=True)
    return center * lax.rsqrt(variance + norm_eps) * gain + shift


def norm_backward(values, gain, shift, upstream):
    result, pullback = jax.vjp(lambda inner: layer_norm(inner, gain, shift), values)
    return pullback(upstream)[0]


def contract_last(left, right):
    return lax.dot_general(
        left, right, (((1,), (1,)), ((), ())), preferred_element_type=jnp.float32
    )


def contract_first(left, right):
    return lax.dot_general(
        left, right, (((0,), (0,)), ((), ())), preferred_element_type=jnp.float32
    )


def project_forward(inputs, weight, down_rows, up_rows):
    reduced = contract_last(inputs, down_rows).astype(jnp.bfloat16)
    output = jnp.dot(inputs, weight, preferred_element_type=jnp.float32)
    output = output + adapter_scale * jnp.dot(reduced, up_rows, preferred_element_type=jnp.float32)
    return (output, reduced)


def projection_backward(upstream, inputs, reduced, weight, down_rows, up_rows):
    reduced_grad = (adapter_scale * contract_last(upstream, up_rows)).astype(jnp.bfloat16)
    input_grad = contract_last(upstream, weight) + jnp.dot(
        reduced_grad, down_rows, preferred_element_type=jnp.float32
    )
    down_grad = contract_first(reduced_grad, inputs)
    up_grad = adapter_scale * contract_first(reduced, upstream)
    return (input_grad, down_grad, up_grad)


def dg(left, right, left_dim, right_dim):
    return lax.dot_general(
        left, right, (((left_dim,), (right_dim,)), ((), ())), preferred_element_type=jnp.float32
    )


def spans(tq, masked, maxp=512):
    out=[]
    for i in range(1024//tq):
        lo=i*tq
        hi=max(lo+tq,maxp) if masked else 1024
        out.append((lo,hi))
    return out
def mask_scores(s, lo, tq, hi, prefix):
    if lo==0: keep,rest=None,s
    else: keep,rest=s[:,:lo],s[:,lo:]
    w=hi-lo
    kp=lax.broadcasted_iota(jnp.int32,(tq,w),1)+lo
    qp=lax.broadcasted_iota(jnp.int32,(tq,w),0)+lo
    rest=jnp.where((kp<=qp)|(kp<prefix),rest,masked_score)
    return rest if keep is None else jnp.concatenate([keep,rest],axis=1)
def fwd_kernel(prefix_ref,q_ref,k_ref,v_ref,o_ref,lse_ref,*,masked,tq):
    prefix=prefix_ref[0] if masked else None
    lane=lax.broadcasted_iota(jnp.int32,(1,128),1)
    k=k_ref[...]; v=v_ref[...]
    for lo,hi in spans(tq,masked):
        q=q_ref[lo:lo+tq,:]*jnp.asarray(0.125,jnp.bfloat16)
        outs=[]
        for h in range(2):
            sel=(lane<64) if h==0 else (lane>=64)
            qh=jnp.where(sel,q,jnp.zeros_like(q))
            s=dg(qh,k[:hi],1,1)
            if masked: s=mask_scores(s,lo,tq,hi,prefix)
            m=jnp.max(s,axis=-1,keepdims=True)
            e=jnp.exp(s-m)
            l=jnp.sum(e,axis=-1,keepdims=True)
            o=dg(e.astype(jnp.bfloat16),v[:hi],1,0)*(1.0/l)
            outs.append(o)
            lse_ref[0,lo:lo+tq,h:h+1]=m+jnp.log(l)
        o_ref[lo:lo+tq,:]=jnp.where(lane<64,outs[0],outs[1]).astype(jnp.bfloat16)
def attn_fwd(q,k,v,prefix,masked,tq=256,pick=(0,0,0)):
    spec=lambda off: pl.BlockSpec((1024,128),lambda i:(0,i+off))
    return pl.pallas_call(functools.partial(fwd_kernel,masked=masked,tq=tq),grid=(8,),
        in_specs=[pl.BlockSpec(memory_space=pltpu.SMEM),spec(pick[0]),spec(pick[1]),spec(pick[2])],
        out_specs=[spec(0),pl.BlockSpec((1,1024,2),lambda i:(i,0,0))],
        out_shape=[jax.ShapeDtypeStruct((1024,1024),jnp.bfloat16),jax.ShapeDtypeStruct((8,1024,2),jnp.float32)],
        name="attn_fwd_%s_%d"%("m" if masked else "f",tq))(prefix,q,k,v)
def bwd_kernel(prefix_ref,q_ref,k_ref,v_ref,do_ref,lse_ref,dq_ref,dk_ref,dv_ref,dkt,dvt,*,masked,tq,mode):
    prefix=prefix_ref[0] if masked else None
    lane=lax.broadcasted_iota(jnp.int32,(1,128),1)
    k=k_ref[...]; v=v_ref[...]
    dkt[...]=jnp.zeros_like(dkt); dvt[...]=jnp.zeros_like(dvt)
    for lo,hi in spans(tq,masked):
        q=q_ref[lo:lo+tq,:]*jnp.asarray(0.125,jnp.bfloat16)
        do=do_ref[lo:lo+tq,:]
        if mode=="wt":
            qt=q.T; dot=do.T
        dqs=[]
        for h in range(2):
            sel=(lane<64) if h==0 else (lane>=64)
            qh=jnp.where(sel,q,jnp.zeros_like(q)); doh=jnp.where(sel,do,jnp.zeros_like(do))
            s=dg(qh,k[:hi],1,1)
            if masked: s=mask_scores(s,lo,tq,hi,prefix)
            p=jnp.exp(s-lse_ref[0,lo:lo+tq,h:h+1])
            dp=dg(doh,v[:hi],1,1)
            d=jnp.sum(p*dp,axis=-1,keepdims=True)
            ds=(p*(dp-d)).astype(jnp.bfloat16)
            pb=p.astype(jnp.bfloat16)
            dqs.append(dg(ds,k[:hi],1,0))
            if mode=="wt":
                r=slice(64*h,64*h+64)
                dvt[r,:hi]+=dg(dot[r],pb,1,0)
                dkt[r,:hi]+=dg(qt[r],ds,1,0)
            else:
                dvt[:hi]+=dg(pb,doh,0,0)
                dkt[:hi]+=dg(ds,qh,0,0)
        dq_ref[lo:lo+tq,:]=(jnp.where(lane<64,dqs[0],dqs[1])*0.125).astype(jnp.bfloat16)
    if mode=="wt":
        dk_ref[...]=dkt[...].T.astype(jnp.bfloat16); dv_ref[...]=dvt[...].T.astype(jnp.bfloat16)
    else:
        dk_ref[...]=dkt[...].astype(jnp.bfloat16); dv_ref[...]=dvt[...].astype(jnp.bfloat16)
def attn_bwd(q,k,v,do,lse,prefix,masked,tq=256,pick=(0,0,0),mode="wt"):
    spec=lambda off: pl.BlockSpec((1024,128),lambda i:(0,i+off))
    acc=(128,1024) if mode=="wt" else (1024,128)
    return pl.pallas_call(functools.partial(bwd_kernel,masked=masked,tq=tq,mode=mode),grid=(8,),
        in_specs=[pl.BlockSpec(memory_space=pltpu.SMEM),spec(pick[0]),spec(pick[1]),spec(pick[2]),spec(0),pl.BlockSpec((1,1024,2),lambda i:(i,0,0))],
        out_specs=[spec(0)]*3,
        out_shape=[jax.ShapeDtypeStruct((1024,1024),jnp.bfloat16)]*3,
        scratch_shapes=[pltpu.VMEM(acc,jnp.float32)]*2,
        name="attn_bwd_%s_%d_%s"%("m" if masked else "f",tq,mode))(prefix,q,k,v,do,lse)


def on_device(
    hidden_in,
    enc_states,
    cotangent,
    prefix_len,
    adapter_ids,
    self_qkv,
    self_out,
    cross_qkv,
    cross_out,
    expand_weight,
    reduce_weight,
    attention_adapters,
    narrow_adapters,
    wide_adapters,
    norm_gains,
    norm_shifts,
):
    hidden = hidden_in[0]
    encoder = enc_states[0]
    upstream = cotangent[0].astype(jnp.float32)
    adapter_slot = adapter_ids[0]
    self_full, self_out_full, self_adapt = (
        lax.all_gather(self_qkv, "shard", axis=1, tiled=True),
        lax.all_gather(self_out, "shard", axis=0, tiled=True),
        lax.all_gather(attention_adapters[:4], "shard", axis=4, tiled=True),
    )
    self_sel = lax.dynamic_index_in_dim(self_adapt, adapter_slot, 2, keepdims=False)
    query_f, query_red = project_forward(hidden, self_full[0], self_sel[0, 0], self_sel[0, 1])
    key_f, key_red = project_forward(hidden, self_full[1], self_sel[1, 0], self_sel[1, 1])
    value_f, value_red = project_forward(hidden, self_full[2], self_sel[2, 0], self_sel[2, 1])
    queries = query_f.astype(jnp.bfloat16)
    keys_in = key_f.astype(jnp.bfloat16)
    values_in = value_f.astype(jnp.bfloat16)
    self_mixed, self_lse = attn_fwd(queries, keys_in, values_in, prefix_len, True)
    self_branch, self_out_red = project_forward(
        self_mixed, self_out_full, self_sel[3, 0], self_sel[3, 1]
    )
    self_sum = hidden.astype(jnp.float32) + self_branch
    after_self = layer_norm(self_sum, norm_gains[0], norm_shifts[0])
    cross_full, cross_out_full, cross_adapt = (
        lax.all_gather(cross_qkv, "shard", axis=1, tiled=True),
        lax.all_gather(cross_out, "shard", axis=0, tiled=True),
        lax.all_gather(attention_adapters[4:], "shard", axis=4, tiled=True),
    )
    cross_sel = lax.dynamic_index_in_dim(cross_adapt, adapter_slot, 2, keepdims=False)
    cross_in = after_self.astype(jnp.bfloat16)
    cquery_f, cquery_red = project_forward(
        cross_in, cross_full[0], cross_sel[0, 0], cross_sel[0, 1]
    )
    ckey_f, ckey_red = project_forward(encoder, cross_full[1], cross_sel[1, 0], cross_sel[1, 1])
    cvalue_f, cvalue_red = project_forward(encoder, cross_full[2], cross_sel[2, 0], cross_sel[2, 1])
    cross_queries = cquery_f.astype(jnp.bfloat16)
    cross_keys = ckey_f.astype(jnp.bfloat16)
    cross_values = cvalue_f.astype(jnp.bfloat16)
    cross_mixed, cross_lse = attn_fwd(
        cross_queries, cross_keys, cross_values, prefix_len, False
    )
    cross_branch, cross_out_red = project_forward(
        cross_mixed, cross_out_full, cross_sel[3, 0], cross_sel[3, 1]
    )
    cross_sum = after_self + cross_branch
    after_cross = layer_norm(cross_sum, norm_gains[1], norm_shifts[1])
    expand_full, reduce_full, narrow_full, wide_full = (
        lax.all_gather(expand_weight, "shard", axis=0, tiled=True),
        lax.all_gather(reduce_weight, "shard", axis=0, tiled=True),
        lax.all_gather(narrow_adapters, "shard", axis=3, tiled=True),
        lax.all_gather(wide_adapters, "shard", axis=3, tiled=True),
    )
    narrow_sel = lax.dynamic_index_in_dim(narrow_full, adapter_slot, 1, keepdims=False)
    wide_sel = lax.dynamic_index_in_dim(wide_full, adapter_slot, 1, keepdims=False)
    feed_in = after_cross.astype(jnp.bfloat16)
    expanded, expand_red = project_forward(feed_in, expand_full, narrow_sel[0], wide_sel[0])
    cdf = 0.5 + 0.5 * lax.erf(expanded * 0.7071067811865476)
    active = (expanded * cdf).astype(jnp.bfloat16)
    slope = cdf + expanded * jnp.exp(-0.5 * expanded * expanded) * 0.3989422804014327
    feed_branch, reduce_red = project_forward(active, reduce_full, wide_sel[1], narrow_sel[1])
    feed_sum = after_cross + feed_branch
    layer_out = layer_norm(feed_sum, norm_gains[2], norm_shifts[2]).astype(jnp.bfloat16)
    expand_reverse, reduce_back, narrow_back, wide_back = (
        lax.all_gather(expand_weight, "shard", axis=0, tiled=True),
        lax.all_gather(reduce_weight, "shard", axis=0, tiled=True),
        lax.all_gather(narrow_adapters, "shard", axis=3, tiled=True),
        lax.all_gather(wide_adapters, "shard", axis=3, tiled=True),
    )
    narrow_bsel = lax.dynamic_index_in_dim(narrow_back, adapter_slot, 1, keepdims=False)
    wide_bsel = lax.dynamic_index_in_dim(wide_back, adapter_slot, 1, keepdims=False)
    grad_feed = norm_backward(feed_sum, norm_gains[2], norm_shifts[2], upstream)
    active_grad, reduce_down_grad, reduce_up_gradient = projection_backward(
        grad_feed.astype(jnp.bfloat16),
        active,
        reduce_red,
        reduce_back,
        wide_bsel[1],
        narrow_bsel[1],
    )
    expanded_grad = (active_grad.astype(jnp.bfloat16).astype(jnp.float32) * slope).astype(
        jnp.bfloat16
    )
    feed_in_grad, expand_down_grad, expand_up_grad = projection_backward(
        expanded_grad, feed_in, expand_red, expand_reverse, narrow_bsel[0], wide_bsel[0]
    )
    after_cross_grad = grad_feed + feed_in_grad
    cross_back, cross_out_back, cross_adapt_back = (
        lax.all_gather(cross_qkv, "shard", axis=1, tiled=True),
        lax.all_gather(cross_out, "shard", axis=0, tiled=True),
        lax.all_gather(attention_adapters[4:], "shard", axis=4, tiled=True),
    )
    cross_bsel = lax.dynamic_index_in_dim(cross_adapt_back, adapter_slot, 2, keepdims=False)
    grad_cross = norm_backward(cross_sum, norm_gains[1], norm_shifts[1], after_cross_grad)
    cross_mixed_grad, cout_down, cout_up = projection_backward(
        grad_cross.astype(jnp.bfloat16),
        cross_mixed,
        cross_out_red,
        cross_out_back,
        cross_bsel[3, 0],
        cross_bsel[3, 1],
    )
    cquery_grad, ckey_grad, cvalue_grad = attn_bwd(
        cross_queries,
        cross_keys,
        cross_values,
        cross_mixed_grad.astype(jnp.bfloat16),
        cross_lse,
        prefix_len,
        False,
    )
    cross_in_grad, cquery_down, cquery_up = projection_backward(
        cquery_grad, cross_in, cquery_red, cross_back[0], cross_bsel[0, 0], cross_bsel[0, 1]
    )
    enc_key_grad, ckey_down, ckey_up = projection_backward(
        ckey_grad, encoder, ckey_red, cross_back[1], cross_bsel[1, 0], cross_bsel[1, 1]
    )
    enc_value_grad, cvalue_down, cvalue_up = projection_backward(
        cvalue_grad, encoder, cvalue_red, cross_back[2], cross_bsel[2, 0], cross_bsel[2, 1]
    )
    encoder_grad = enc_key_grad + enc_value_grad
    after_self_grad = grad_cross + cross_in_grad
    self_back, self_out_back, self_adapt_back = (
        lax.all_gather(self_qkv, "shard", axis=1, tiled=True),
        lax.all_gather(self_out, "shard", axis=0, tiled=True),
        lax.all_gather(attention_adapters[:4], "shard", axis=4, tiled=True),
    )
    self_bsel = lax.dynamic_index_in_dim(self_adapt_back, adapter_slot, 2, keepdims=False)
    grad_self = norm_backward(self_sum, norm_gains[0], norm_shifts[0], after_self_grad)
    self_mixed_grad, sout_down, sout_up = projection_backward(
        grad_self.astype(jnp.bfloat16),
        self_mixed,
        self_out_red,
        self_out_back,
        self_bsel[3, 0],
        self_bsel[3, 1],
    )
    query_grad, key_grad, value_grad = attn_bwd(
        queries,
        keys_in,
        values_in,
        self_mixed_grad.astype(jnp.bfloat16),
        self_lse,
        prefix_len,
        True,
    )
    hid_query, squery_down, squery_up = projection_backward(
        query_grad, hidden, query_red, self_back[0], self_bsel[0, 0], self_bsel[0, 1]
    )
    hidden_key_rows, self_key_down, self_key_up = projection_backward(
        key_grad, hidden, key_red, self_back[1], self_bsel[1, 0], self_bsel[1, 1]
    )
    hid_value, svalue_down, svalue_up = projection_backward(
        value_grad, hidden, value_red, self_back[2], self_bsel[2, 0], self_bsel[2, 1]
    )
    hidden_grad = grad_self + hid_query + hidden_key_rows + hid_value
    attention_parts = (
        (squery_down, squery_up),
        (self_key_down, self_key_up),
        (svalue_down, svalue_up),
        (sout_down, sout_up),
        (cquery_down, cquery_up),
        (ckey_down, ckey_up),
        (cvalue_down, cvalue_up),
        (cout_down, cout_up),
    )
    attention_stack = jnp.stack(
        [jnp.stack([down_part, up_part]) for down_part, up_part in attention_parts]
    )
    narrow_stack = jnp.stack([expand_down_grad, reduce_up_gradient])
    wide_stack = jnp.stack([expand_up_grad, reduce_down_grad])
    adapter_slot_count = attention_adapters.shape[2]
    rank_rows = attention_stack.shape[2]
    attention_fragment = attention_stack.reshape(1, 16, rank_rows, attention_stack.shape[3])
    received = (
        lax.all_to_all(
            attention_fragment.astype(jnp.bfloat16),
            "shard",
            split_axis=3,
            concat_axis=0,
            tiled=True,
        ).astype(attention_fragment.dtype),
        lax.all_to_all(
            narrow_stack[None].astype(jnp.bfloat16),
            "shard",
            split_axis=3,
            concat_axis=0,
            tiled=True,
        ).astype(jnp.float32),
        lax.all_to_all(
            wide_stack[None].astype(jnp.bfloat16), "shard", split_axis=3, concat_axis=0, tiled=True
        ).astype(jnp.float32),
    )
    group_ids = lax.all_gather(adapter_ids, "shard", axis=0, tiled=True)
    one_hot = (
        group_ids[:, None] == jnp.arange(adapter_slot_count, dtype=jnp.int32)[None, :]
    ).astype(jnp.float32)
    selector = one_hot[:, None, :, None, None]
    owned_attention = jnp.sum(selector * received[0][:, :, None], axis=0)
    owned_attention = owned_attention.reshape(
        8, 2, adapter_slot_count, rank_rows, owned_attention.shape[3]
    )
    owned_narrow = jnp.sum(selector * received[1][:, :, None], axis=0)
    owned_wide = jnp.sum(selector * received[2][:, :, None], axis=0)
    attention_grad, narrow_grad, wide_grad = (
        lax.psum(owned_attention.astype(jnp.bfloat16), "rep").astype(jnp.float32),
        lax.psum(owned_narrow.astype(jnp.bfloat16), "rep").astype(jnp.float32),
        lax.psum(owned_wide.astype(jnp.bfloat16), "rep").astype(jnp.float32),
    )
    return (
        layer_out[None],
        hidden_grad[None],
        encoder_grad[None],
        attention_grad,
        narrow_grad,
        wide_grad,
    )


def solution(mesh):
    in_specs = (
        P(("shard", "rep"), None, None),
        P(("shard", "rep"), None, None),
        P(("shard", "rep"), None, None),
        P(("shard", "rep")),
        P(("shard", "rep")),
        P(None, "shard", None),
        P("shard", None),
        P(None, "shard", None),
        P("shard", None),
        P("shard", None),
        P("shard", None),
        P(None, None, None, None, "shard"),
        P(None, None, None, "shard"),
        P(None, None, None, "shard"),
        P(),
        P(),
    )
    out_specs = (
        P(("shard", "rep"), None, None),
        P(("shard", "rep"), None, None),
        P(("shard", "rep"), None, None),
        P(None, None, None, None, "shard"),
        P(None, None, None, "shard"),
        P(None, None, None, "shard"),
    )
    return jax.shard_map(
        on_device, mesh=mesh, in_specs=in_specs, out_specs=out_specs, check_vma=False
    )
```

```python
import functools

import jax
import jax.numpy as jnp
from jax import lax
from jax.experimental import pallas as pl
from jax.experimental.pallas import tpu as pltpu
from jax.sharding import PartitionSpec as P

HEADS = 16
HEAD_DIM = 64


adapter_scale = 2.0
norm_eps = 1e-05
masked_score = -1000000000.0


def layer_norm(values, gain, shift):
    center = values - jnp.mean(values, axis=-1, keepdims=True)
    variance = jnp.mean(center * center, axis=-1, keepdims=True)
    return center * lax.rsqrt(variance + norm_eps) * gain + shift


def norm_backward(values, gain, shift, upstream):
    result, pullback = jax.vjp(lambda inner: layer_norm(inner, gain, shift), values)
    return pullback(upstream)[0]


def contract_last(left, right):
    return lax.dot_general(
        left, right, (((1,), (1,)), ((), ())), preferred_element_type=jnp.float32
    )


def contract_first(left, right):
    return lax.dot_general(
        left, right, (((0,), (0,)), ((), ())), preferred_element_type=jnp.float32
    )


def project_forward(inputs, weight, down_rows, up_rows):
    reduced = contract_last(inputs, down_rows).astype(jnp.bfloat16)
    output = jnp.dot(inputs, weight, preferred_element_type=jnp.float32)
    output = output + adapter_scale * jnp.dot(reduced, up_rows, preferred_element_type=jnp.float32)
    return (output, reduced)


def projection_backward(upstream, inputs, reduced, weight, down_rows, up_rows):
    reduced_grad = (adapter_scale * contract_last(upstream, up_rows)).astype(jnp.bfloat16)
    input_grad = contract_last(upstream, weight) + jnp.dot(
        reduced_grad, down_rows, preferred_element_type=jnp.float32
    )
    down_grad = contract_first(reduced_grad, inputs)
    up_grad = adapter_scale * contract_first(reduced, upstream)
    return (input_grad, down_grad, up_grad)


def dg(left, right, left_dim, right_dim):
    return lax.dot_general(
        left, right, (((left_dim,), (right_dim,)), ((), ())), preferred_element_type=jnp.float32
    )


def spans(tq, masked, maxp=512):
    out=[]
    for i in range(1024//tq):
        lo=i*tq
        hi=max(lo+tq,maxp) if masked else 1024
        out.append((lo,hi))
    return out
def mask_scores(s, lo, tq, hi, prefix):
    if lo==0: keep,rest=None,s
    else: keep,rest=s[:,:lo],s[:,lo:]
    w=hi-lo
    kp=lax.broadcasted_iota(jnp.int32,(tq,w),1)+lo
    qp=lax.broadcasted_iota(jnp.int32,(tq,w),0)+lo
    rest=jnp.where((kp<=qp)|(kp<prefix),rest,masked_score)
    return rest if keep is None else jnp.concatenate([keep,rest],axis=1)
def fwd_kernel(prefix_ref,q_ref,k_ref,v_ref,o_ref,lse_ref,*,masked,tq):
    prefix=prefix_ref[0] if masked else None
    lane=lax.broadcasted_iota(jnp.int32,(1,128),1)
    k=k_ref[...]; v=v_ref[...]
    for lo,hi in spans(tq,masked):
        q=q_ref[lo:lo+tq,:]*jnp.asarray(0.125,jnp.bfloat16)
        outs=[]
        for h in range(2):
            sel=(lane<64) if h==0 else (lane>=64)
            qh=jnp.where(sel,q,jnp.zeros_like(q))
            s=dg(qh,k[:hi],1,1)
            if masked: s=mask_scores(s,lo,tq,hi,prefix)
            m=jnp.max(s,axis=-1,keepdims=True)
            e=jnp.exp(s-m)
            l=jnp.sum(e,axis=-1,keepdims=True)
            o=dg(e.astype(jnp.bfloat16),v[:hi],1,0)*(1.0/l)
            outs.append(o)
            lse_ref[0,lo:lo+tq,h:h+1]=m+jnp.log(l)
        o_ref[lo:lo+tq,:]=jnp.where(lane<64,outs[0],outs[1]).astype(jnp.bfloat16)
def attn_fwd(q,k,v,prefix,masked,tq=256,pick=(0,0,0)):
    spec=lambda off: pl.BlockSpec((1024,128),lambda i:(0,i+off))
    return pl.pallas_call(functools.partial(fwd_kernel,masked=masked,tq=tq),grid=(8,),
        in_specs=[pl.BlockSpec(memory_space=pltpu.SMEM),spec(pick[0]),spec(pick[1]),spec(pick[2])],
        out_specs=[spec(0),pl.BlockSpec((1,1024,2),lambda i:(i,0,0))],
        out_shape=[jax.ShapeDtypeStruct((1024,1024),jnp.bfloat16),jax.ShapeDtypeStruct((8,1024,2),jnp.float32)],
        name="attn_fwd_%s_%d"%("m" if masked else "f",tq))(prefix,q,k,v)
def bwd_kernel(prefix_ref,q_ref,k_ref,v_ref,do_ref,lse_ref,dq_ref,dk_ref,dv_ref,dkt,dvt,*,masked,tq,mode):
    prefix=prefix_ref[0] if masked else None
    lane=lax.broadcasted_iota(jnp.int32,(1,128),1)
    k=k_ref[...]; v=v_ref[...]
    dkt[...]=jnp.zeros_like(dkt); dvt[...]=jnp.zeros_like(dvt)
    for lo,hi in spans(tq,masked):
        q=q_ref[lo:lo+tq,:]*jnp.asarray(0.125,jnp.bfloat16)
        do=do_ref[lo:lo+tq,:]
        if mode=="wt":
            qt=q.T; dot=do.T
        dqs=[]
        for h in range(2):
            sel=(lane<64) if h==0 else (lane>=64)
            qh=jnp.where(sel,q,jnp.zeros_like(q)); doh=jnp.where(sel,do,jnp.zeros_like(do))
            s=dg(qh,k[:hi],1,1)
            if masked: s=mask_scores(s,lo,tq,hi,prefix)
            p=jnp.exp(s-lse_ref[0,lo:lo+tq,h:h+1])
            dp=dg(doh,v[:hi],1,1)
            d=jnp.sum(p*dp,axis=-1,keepdims=True)
            ds=(p*(dp-d)).astype(jnp.bfloat16)
            pb=p.astype(jnp.bfloat16)
            dqs.append(dg(ds,k[:hi],1,0))
            if mode=="wt":
                r=slice(64*h,64*h+64)
                dvt[r,:hi]+=dg(dot[r],pb,1,0)
                dkt[r,:hi]+=dg(qt[r],ds,1,0)
            else:
                dvt[:hi]+=dg(pb,doh,0,0)
                dkt[:hi]+=dg(ds,qh,0,0)
        dq_ref[lo:lo+tq,:]=(jnp.where(lane<64,dqs[0],dqs[1])*0.125).astype(jnp.bfloat16)
    if mode=="wt":
        dk_ref[...]=dkt[...].T.astype(jnp.bfloat16); dv_ref[...]=dvt[...].T.astype(jnp.bfloat16)
    else:
        dk_ref[...]=dkt[...].astype(jnp.bfloat16); dv_ref[...]=dvt[...].astype(jnp.bfloat16)
def attn_bwd(q,k,v,do,lse,prefix,masked,tq=256,pick=(0,0,0),mode="wt"):
    spec=lambda off: pl.BlockSpec((1024,128),lambda i:(0,i+off))
    acc=(128,1024) if mode=="wt" else (1024,128)
    return pl.pallas_call(functools.partial(bwd_kernel,masked=masked,tq=tq,mode=mode),grid=(8,),
        in_specs=[pl.BlockSpec(memory_space=pltpu.SMEM),spec(pick[0]),spec(pick[1]),spec(pick[2]),spec(0),pl.BlockSpec((1,1024,2),lambda i:(i,0,0))],
        out_specs=[spec(0)]*3,
        out_shape=[jax.ShapeDtypeStruct((1024,1024),jnp.bfloat16)]*3,
        scratch_shapes=[pltpu.VMEM(acc,jnp.float32)]*2,
        name="attn_bwd_%s_%d_%s"%("m" if masked else "f",tq,mode))(prefix,q,k,v,do,lse)


def select_kernel(ids_ref, att_ref, nar_ref, wide_ref, thin_out, wide_out):
    thin_out[0, :16] = att_ref[:, 0]
    thin_out[0, 16:] = nar_ref[:, 0]
    wide_out[0] = wide_ref[:, 0]


def select_rows(group_ids, attention_adapters, narrow_adapters, wide_adapters):
    count = group_ids.shape[0]
    slots, rank, width = attention_adapters.shape[2:]
    wide = wide_adapters.shape[3]
    flat = attention_adapters.reshape(16, slots, rank, width)
    pick = lambda dest, ids: (0, ids[dest], 0, 0)
    place = lambda dest, ids: (dest, 0, 0, 0)
    return pl.pallas_call(
        select_kernel,
        grid_spec=pltpu.PrefetchScalarGridSpec(
            num_scalar_prefetch=1,
            grid=(count,),
            in_specs=[
                pl.BlockSpec((16, 1, rank, width), pick),
                pl.BlockSpec((2, 1, rank, width), pick),
                pl.BlockSpec((2, 1, rank, wide), pick),
            ],
            out_specs=[
                pl.BlockSpec((1, 18, rank, width), place),
                pl.BlockSpec((1, 2, rank, wide), place),
            ],
        ),
        out_shape=[
            jax.ShapeDtypeStruct((count, 18, rank, width), jnp.bfloat16),
            jax.ShapeDtypeStruct((count, 2, rank, wide), jnp.bfloat16),
        ],
        name="select_rows",
    )(group_ids, flat, narrow_adapters, wide_adapters)


def exchange(rows):
    return lax.all_to_all(rows, "shard", split_axis=0, concat_axis=0, tiled=True)


def join_columns(pieces):
    count, blocks, rank, width = pieces.shape
    return pieces.transpose(1, 2, 0, 3).reshape(blocks, rank, count * width)


def split_columns(parts, count):
    stack = jnp.stack(parts).astype(jnp.bfloat16)
    blocks, rank, width = stack.shape
    return stack.reshape(blocks, rank, count, width // count).transpose(2, 0, 1, 3)


def sum_slots(received, selector):
    picked = selector[:, None, :, None, None] * received.astype(jnp.float32)[:, :, None]
    return jnp.sum(picked, axis=0).astype(jnp.bfloat16)


def on_device(
    hidden_in,
    enc_states,
    cotangent,
    prefix_len,
    adapter_ids,
    self_qkv,
    self_out,
    cross_qkv,
    cross_out,
    expand_weight,
    reduce_weight,
    attention_adapters,
    narrow_adapters,
    wide_adapters,
    norm_gains,
    norm_shifts,
):
    hidden = hidden_in[0]
    encoder = enc_states[0]
    upstream = cotangent[0].astype(jnp.float32)
    slot_count = attention_adapters.shape[2]
    self_full = lax.all_gather(self_qkv, "shard", axis=1, tiled=True)
    group_ids = lax.all_gather(adapter_ids, "shard", axis=0, tiled=True)
    group_size = group_ids.shape[0]
    thin_pick, wide_pick = select_rows(
        group_ids, attention_adapters, narrow_adapters, wide_adapters
    )
    thin_rows = join_columns(exchange(thin_pick))
    wide_rows = join_columns(exchange(wide_pick))
    middle = jnp.concatenate([cross_qkv, self_out[None], cross_out[None]], axis=0)
    middle_full = lax.all_gather(middle, "shard", axis=1, tiled=True)
    cross_full = middle_full[:3]
    self_out_full = middle_full[3]
    cross_out_full = middle_full[4]
    expand_full = lax.all_gather(expand_weight, "shard", axis=0, tiled=True)
    reduce_full = lax.all_gather(reduce_weight, "shard", axis=0, tiled=True)
    self_sel = thin_rows[:8].reshape(4, 2, *thin_rows.shape[1:])
    cross_sel = thin_rows[8:16].reshape(4, 2, *thin_rows.shape[1:])
    narrow_sel = thin_rows[16:]
    wide_sel = wide_rows
    query_f, query_red = project_forward(hidden, self_full[0], self_sel[0, 0], self_sel[0, 1])
    key_f, key_red = project_forward(hidden, self_full[1], self_sel[1, 0], self_sel[1, 1])
    value_f, value_red = project_forward(hidden, self_full[2], self_sel[2, 0], self_sel[2, 1])
    queries = query_f.astype(jnp.bfloat16)
    keys_in = key_f.astype(jnp.bfloat16)
    values_in = value_f.astype(jnp.bfloat16)
    self_mixed, self_lse = attn_fwd(queries, keys_in, values_in, prefix_len, True)
    self_branch, self_out_red = project_forward(
        self_mixed, self_out_full, self_sel[3, 0], self_sel[3, 1]
    )
    self_sum = hidden.astype(jnp.float32) + self_branch
    after_self = layer_norm(self_sum, norm_gains[0], norm_shifts[0])
    cross_in = after_self.astype(jnp.bfloat16)
    cquery_f, cquery_red = project_forward(
        cross_in, cross_full[0], cross_sel[0, 0], cross_sel[0, 1]
    )
    ckey_f, ckey_red = project_forward(encoder, cross_full[1], cross_sel[1, 0], cross_sel[1, 1])
    cvalue_f, cvalue_red = project_forward(encoder, cross_full[2], cross_sel[2, 0], cross_sel[2, 1])
    cross_queries = cquery_f.astype(jnp.bfloat16)
    cross_keys = ckey_f.astype(jnp.bfloat16)
    cross_values = cvalue_f.astype(jnp.bfloat16)
    cross_mixed, cross_lse = attn_fwd(
        cross_queries, cross_keys, cross_values, prefix_len, False
    )
    cross_branch, cross_out_red = project_forward(
        cross_mixed, cross_out_full, cross_sel[3, 0], cross_sel[3, 1]
    )
    cross_sum = after_self + cross_branch
    after_cross = layer_norm(cross_sum, norm_gains[1], norm_shifts[1])
    feed_in = after_cross.astype(jnp.bfloat16)
    expanded, expand_red = project_forward(feed_in, expand_full, narrow_sel[0], wide_sel[0])
    cdf = 0.5 + 0.5 * lax.erf(expanded * 0.7071067811865476)
    active = (expanded * cdf).astype(jnp.bfloat16)
    slope = cdf + expanded * jnp.exp(-0.5 * expanded * expanded) * 0.3989422804014327
    feed_branch, reduce_red = project_forward(active, reduce_full, wide_sel[1], narrow_sel[1])
    feed_sum = after_cross + feed_branch
    layer_out = layer_norm(feed_sum, norm_gains[2], norm_shifts[2]).astype(jnp.bfloat16)
    grad_feed = norm_backward(feed_sum, norm_gains[2], norm_shifts[2], upstream)
    active_grad, reduce_down_grad, reduce_up_gradient = projection_backward(
        grad_feed.astype(jnp.bfloat16),
        active,
        reduce_red,
        reduce_full,
        wide_sel[1],
        narrow_sel[1],
    )
    expanded_grad = (active_grad.astype(jnp.bfloat16).astype(jnp.float32) * slope).astype(
        jnp.bfloat16
    )
    feed_in_grad, expand_down_grad, expand_up_grad = projection_backward(
        expanded_grad, feed_in, expand_red, expand_full, narrow_sel[0], wide_sel[0]
    )
    after_cross_grad = grad_feed + feed_in_grad
    grad_cross = norm_backward(cross_sum, norm_gains[1], norm_shifts[1], after_cross_grad)
    cross_mixed_grad, cout_down, cout_up = projection_backward(
        grad_cross.astype(jnp.bfloat16),
        cross_mixed,
        cross_out_red,
        cross_out_full,
        cross_sel[3, 0],
        cross_sel[3, 1],
    )
    selector = (
        group_ids[:, None] == jnp.arange(slot_count, dtype=jnp.int32)[None, :]
    ).astype(jnp.float32)
    feed_send = [cout_down, cout_up, expand_down_grad, reduce_up_gradient]
    feed_thin = exchange(split_columns(feed_send, group_size))
    feed_wide = exchange(split_columns([expand_up_grad, reduce_down_grad], group_size))
    feed_parts = (sum_slots(feed_thin, selector), sum_slots(feed_wide, selector))
    cross_mixed_low, feed_parts = lax.optimization_barrier(
        (cross_mixed_grad.astype(jnp.bfloat16), feed_parts)
    )
    feed_sums = lax.psum(feed_parts, "rep")
    cquery_grad, ckey_grad, cvalue_grad = attn_bwd(
        cross_queries,
        cross_keys,
        cross_values,
        cross_mixed_low,
        cross_lse,
        prefix_len,
        False,
    )
    cquery_grad, ckey_grad, cvalue_grad, feed_sums = lax.optimization_barrier(
        (cquery_grad, ckey_grad, cvalue_grad, feed_sums)
    )
    cross_in_grad, cquery_down, cquery_up = projection_backward(
        cquery_grad, cross_in, cquery_red, cross_full[0], cross_sel[0, 0], cross_sel[0, 1]
    )
    enc_key_grad, ckey_down, ckey_up = projection_backward(
        ckey_grad, encoder, ckey_red, cross_full[1], cross_sel[1, 0], cross_sel[1, 1]
    )
    enc_value_grad, cvalue_down, cvalue_up = projection_backward(
        cvalue_grad, encoder, cvalue_red, cross_full[2], cross_sel[2, 0], cross_sel[2, 1]
    )
    encoder_grad = enc_key_grad + enc_value_grad
    after_self_grad = grad_cross + cross_in_grad
    grad_self = norm_backward(self_sum, norm_gains[0], norm_shifts[0], after_self_grad)
    self_mixed_grad, sout_down, sout_up = projection_backward(
        grad_self.astype(jnp.bfloat16),
        self_mixed,
        self_out_red,
        self_out_full,
        self_sel[3, 0],
        self_sel[3, 1],
    )
    cross_send = [
        sout_down,
        sout_up,
        cquery_down,
        cquery_up,
        ckey_down,
        ckey_up,
        cvalue_down,
        cvalue_up,
    ]
    cross_part = sum_slots(exchange(split_columns(cross_send, group_size)), selector)
    self_mixed_low, cross_part, encoder_grad = lax.optimization_barrier(
        (self_mixed_grad.astype(jnp.bfloat16), cross_part, encoder_grad)
    )
    cross_sum_rep = lax.psum(cross_part, "rep")
    query_grad, key_grad, value_grad = attn_bwd(
        queries,
        keys_in,
        values_in,
        self_mixed_low,
        self_lse,
        prefix_len,
        True,
    )
    query_grad, key_grad, value_grad, cross_sum_rep = lax.optimization_barrier(
        (query_grad, key_grad, value_grad, cross_sum_rep)
    )
    hid_query, squery_down, squery_up = projection_backward(
        query_grad, hidden, query_red, self_full[0], self_sel[0, 0], self_sel[0, 1]
    )
    hidden_key_rows, self_key_down, self_key_up = projection_backward(
        key_grad, hidden, key_red, self_full[1], self_sel[1, 0], self_sel[1, 1]
    )
    hid_value, svalue_down, svalue_up = projection_backward(
        value_grad, hidden, value_red, self_full[2], self_sel[2, 0], self_sel[2, 1]
    )
    hidden_grad = grad_self + hid_query + hidden_key_rows + hid_value
    late_thin = exchange(
        split_columns(
            [squery_down, squery_up, self_key_down, self_key_up, svalue_down, svalue_up],
            group_size,
        )
    )
    late_sum = lax.psum(sum_slots(late_thin, selector), "rep")
    attention_grad = (
        jnp.concatenate([late_sum, cross_sum_rep, feed_sums[0][:2]], axis=0)
        .astype(jnp.float32)
        .reshape(attention_adapters.shape)
    )
    narrow_grad = feed_sums[0][2:].astype(jnp.float32)
    wide_grad = feed_sums[1].astype(jnp.float32)
    return (
        layer_out[None],
        hidden_grad[None],
        encoder_grad[None],
        attention_grad,
        narrow_grad,
        wide_grad,
    )


def solution(mesh):
    in_specs = (
        P(("shard", "rep"), None, None),
        P(("shard", "rep"), None, None),
        P(("shard", "rep"), None, None),
        P(("shard", "rep")),
        P(("shard", "rep")),
        P(None, "shard", None),
        P("shard", None),
        P(None, "shard", None),
        P("shard", None),
        P("shard", None),
        P("shard", None),
        P(None, None, None, None, "shard"),
        P(None, None, None, "shard"),
        P(None, None, None, "shard"),
        P(),
        P(),
    )
    out_specs = (
        P(("shard", "rep"), None, None),
        P(("shard", "rep"), None, None),
        P(("shard", "rep"), None, None),
        P(None, None, None, None, "shard"),
        P(None, None, None, "shard"),
        P(None, None, None, "shard"),
    )
    return jax.shard_map(
        on_device, mesh=mesh, in_specs=in_specs, out_specs=out_specs, check_vma=False
    )
```
